32 devices in a mesh: group: 4 (over z), dev: 8 (over y, x, core).
Axes of the slice: x: 2, y: 2, z: 4, core: 2. Of those that a mesh axis runs over, the one named last changes fastest.
Arguments:
- field_now: float32 [2, 256, 256, 256], P(None, 'group', 'dev'), may hold values from -6 to 6
- source: float32 [2, 256, 256, 256], P(None, 'group', 'dev'), may hold values from -6 to 6
- wavenumber_sq: float32 [256, 256, 256], P('group', 'dev'), may hold values from 0.02 to 0.2
- shift_sq: float32 [1], replicated, may hold values from 0.05 to 0.2
Outputs:
- field_next: float32 [2, 256, 256, 256], P(None, 'group', 'dev')
The draws below stay inside these ranges and needn't reach their ends.
All inputs are finite; a program needn't handle non-finite values.
Results may differ from the reference program's by a relative error of at most 0.000092.
Values sent between devices are 32-bit elements; how exact they have to be, the bound alone decides.
No kernel may reach another device: no remote copies, remote signals or barrier semaphores. Data moves between devices by JAX's collectives and lax.ppermute only.
A program may use at most 128 MiB of HBM per device.

```python
import math
import jax
import jax.numpy as jnp
from jax import lax

NZ = 256
SWEEPS = 3
NX = 256
NY = 256


def level_of(stream_key, shape, split, low, high):
    def one(position, shards_of):
        draws = jax.random.uniform(jax.random.fold_in(jax.random.fold_in(stream_key, 6), position), (shards_of,), jnp.float32, low / len(split), high / len(split))
        return jnp.repeat(jnp.exp(draws), shape[position] // shards_of).reshape((-1,) + (1,) * (len(shape) - position - 1))

    gain = one(*split[0])
    for cut in split[1:]:
        gain = gain * one(*cut)
    return gain


def bell_draw(key, dims, width, most, cuts=(), kind=jnp.bfloat16):
    loudness = level_of(key, dims, cuts, -0.22, 0.18) if cuts else 1.0
    result = jax.random.normal(key, dims, jnp.float32) * width * loudness
    return jnp.minimum(jnp.maximum(result, -most), most).astype(kind)


def setup_inputs(seed: int = 0) -> dict:
    key_of = jax.random.split(jax.random.key(seed), 5)
    return {
        "field_now": bell_draw(key_of[0], (2, NX, NY, NZ), 1.0, 6.0, ((1, 4), (2, 8)), jnp.float32),
        "source": bell_draw(key_of[1], (2, NX, NY, NZ), 1.0, 6.0, ((1, 4), (2, 8)), jnp.float32),
        "wavenumber_sq": jnp.clip(jnp.exp(math.log(0.2) - 2.3025851 * jax.random.uniform(key_of[2], (NX, NY, NZ), jnp.float32) ** level_of(key_of[2], (NX, NY, NZ), ((0, 4), (1, 8)), -0.2, 0.2)), 0.02, 0.2),
        "shift_sq": jnp.clip(jax.random.uniform(key_of[3], (1,), jnp.float32, 0.05, 0.2), 0.05, 0.2),
    }


RELAX = 0.8
DAMPING = 0.5
HIGHEST = lax.Precision.HIGHEST

def operate(padded, wave_sq):
    centre = padded[:, 1:-1, 1:-1, :]
    beside = padded[:, 2:, 1:-1, :] + padded[:, :-2, 1:-1, :]
    beside = beside + padded[:, 1:-1, 2:, :] + padded[:, 1:-1, :-2, :]
    vertical = jnp.pad(centre, ((0, 0), (0, 0), (0, 0), (1, 1)))
    beside = beside + vertical[..., 2:] + vertical[..., :-2]
    layers = centre.shape[-1]
    height = lax.broadcasted_iota(jnp.int32, (1, 1, layers), 2)
    boundary = jnp.logical_or(height == 0, height == layers - 1).astype(wave_sq.dtype)
    absorb = jnp.sqrt(wave_sq)
    robin = jnp.stack([centre[0] - absorb * centre[1], centre[1] + absorb * centre[0]]) * boundary
    return (6.0 - wave_sq) * centre - beside - robin

def fourier_table(count, sign, real_type):
    index_row = lax.broadcasted_iota(jnp.int32, (count, count), 0)
    index_col = lax.broadcasted_iota(jnp.int32, (count, count), 1)
    angle = 2.0 * math.pi / count * (index_row * index_col % count).astype(real_type)
    cosine = jnp.cos(angle)
    sine = sign * jnp.sin(angle)
    scale = 1.0 if sign < 0 else 1.0 / count
    return scale * jnp.stack([jnp.stack([cosine, sine]), jnp.stack([-sine, cosine])])

def vertical_basis(layers, real_type):
    index_row = lax.broadcasted_iota(jnp.int32, (layers, layers), 0) + 1
    index_col = lax.broadcasted_iota(jnp.int32, (layers, layers), 1) + 1
    angle = math.pi / (layers + 1) * (index_row * index_col % (2 * (layers + 1))).astype(real_type)
    return math.sqrt(2.0 / (layers + 1)) * jnp.sin(angle)

def horizontal_eigen(wave_index, count, real_type):
    angle = 2.0 * math.pi / count * wave_index.astype(real_type)
    return (2.0 - 2.0 * jnp.cos(angle)) / 16.0

def vertical_eigen(mode_index, layers, real_type):
    angle = math.pi / (layers + 1) * (mode_index + 1).astype(real_type)
    return 2.0 - 2.0 * jnp.cos(angle)

def divide_modes(modes, eigen, shift):
    real_part = eigen - shift
    imag_part = -DAMPING * shift
    modulus = real_part * real_part + imag_part * imag_part
    upper = (modes[0] * real_part + modes[1] * imag_part) / modulus
    lower = (modes[1] * real_part - modes[0] * imag_part) / modulus
    return jnp.stack([upper, lower])

def restrict(residual):
    extent = residual.shape
    blocks = residual.reshape(2, extent[1] // 4, 4, extent[2] // 4, 4, extent[3])
    return lax.optimization_barrier(jnp.mean(blocks, axis=(2, 4)))

def prolong(coarse):
    extent = coarse.shape
    spread = jnp.broadcast_to(coarse[:, :, None, :, None, :], (2, extent[1], 4, extent[2], 4, extent[3]))
    return spread.reshape(2, extent[1] * 4, extent[2] * 4, extent[3])

def coarse_solve(coarse, shift):
    real_type = coarse.dtype
    waves_x = coarse.shape[1]
    waves_y = coarse.shape[2]
    layers = coarse.shape[3]
    basis = vertical_basis(layers, real_type)
    modes = jnp.einsum('cxyz,zm->cmxy', coarse, basis, precision=HIGHEST)
    modes = jnp.einsum('cmxy,cdyk->dmxk', modes, fourier_table(waves_y, -1, real_type), precision=HIGHEST)
    modes = jnp.einsum('cmxk,cdxj->dmjk', modes, fourier_table(waves_x, -1, real_type), precision=HIGHEST)
    mode_index = lax.broadcasted_iota(jnp.int32, (layers, 1, 1), 0)
    wave_x = lax.broadcasted_iota(jnp.int32, (1, waves_x, 1), 1)
    wave_y = lax.broadcasted_iota(jnp.int32, (1, 1, waves_y), 2)
    eigen = vertical_eigen(mode_index, layers, real_type) + horizontal_eigen(wave_x, waves_x, real_type) + horizontal_eigen(wave_y, waves_y, real_type)
    modes = divide_modes(modes, eigen, shift)
    modes = jnp.einsum('cmjk,cdjx->dmxk', modes, fourier_table(waves_x, 1, real_type), precision=HIGHEST)
    modes = jnp.einsum('cmxk,cdky->dmxy', modes, fourier_table(waves_y, 1, real_type), precision=HIGHEST)
    return jnp.einsum('cmxy,mz->cxyz', modes, basis, precision=HIGHEST)

def reference(field_now, source, wavenumber_sq, shift_sq):
    padded = jnp.pad(field_now, ((0, 0), (1, 1), (1, 1), (0, 0)))
    residual = source - operate(padded, wavenumber_sq)
    correction = coarse_solve(restrict(residual), shift_sq[0])
    field = field_now + prolong(correction)
    weight = RELAX / (6.0 - wavenumber_sq)
    for sweep_index in range(SWEEPS):
        padded = jnp.pad(field, ((0, 0), (1, 1), (1, 1), (0, 0)))
        field = field + weight * (source - operate(padded, wavenumber_sq))
    return field
```

```python
import functools
import math

import jax
import jax.numpy as jnp
import numpy as np
from jax import lax
from jax.experimental import pallas as pl
from jax.experimental.pallas import tpu as pltpu
from jax.sharding import PartitionSpec as P

SWEEPS = 3
RELAX = 0.8
DAMPING = 0.5
HIGHEST = lax.Precision.HIGHEST
BLOCK = 4
LANES = 128
SUBS = 8
HALF = LANES // 2
FIELD_HALO = 3
DATA_HALO = 2
SLABS = 2 * FIELD_HALO + 3 * DATA_HALO
VMEM_LIMIT = 48 * 1024 * 1024

VMEM = pltpu.VMEM
ANY = pl.ANY


def vertical_basis(layers):
    index = np.arange(1, layers + 1, dtype=np.float64)
    return np.sqrt(2.0 / (layers + 1)) * np.sin(np.pi * np.outer(index, index) / (layers + 1))


def cell_order(cells_x, cells_y):
    own = [(x, y) for x in range(cells_x) for y in range(cells_y)]
    rim = [(-1, y) for y in range(cells_y)] + [(cells_x, y) for y in range(cells_y)]
    rim += [(x, -1) for x in range(cells_x)] + [(x, cells_y) for x in range(cells_x)]
    rim += [(-1, -1), (-1, cells_y), (cells_x, -1), (cells_x, cells_y)]
    return np.array(own), np.array(rim)


def spectral_tables(groups, members, cells_x, cells_y, layers):
    own, rim = cell_order(cells_x, cells_y)
    waves_x, waves_y = groups * cells_x, members * cells_y
    high = np.array([(a, b) for a in range(cells_x) for b in range(cells_y)])

    def phase(cells):
        return (
            2.0 * np.pi * np.outer(cells[:, 0], high[:, 0]) / cells_x
            + 2.0 * np.pi * np.outer(cells[:, 1], high[:, 1]) / cells_y
        )

    def packed(cells, inverse):
        angle = phase(cells)
        cos, sin = np.cos(angle), np.sin(angle)
        if inverse:
            scale = 1.0 / (waves_x * waves_y)
            re = scale * np.concatenate([cos.T, -sin.T])
            im = scale * np.concatenate([sin.T, cos.T])
            return re, im
        re = np.concatenate([cos, -sin], axis=1)
        im = np.concatenate([sin, cos], axis=1)
        return re, im

    own_re, own_im = packed(own, False)
    rim_re, rim_im = packed(rim, False)
    pad = np.zeros((HALF - len(rim), own_re.shape[1]))
    forward = np.concatenate([own_re, own_im, rim_re, pad, rim_im, pad])
    own_re, own_im = packed(own, True)
    rim_re, rim_im = packed(rim, True)
    pad = np.zeros((own_re.shape[0], HALF - len(rim)))
    backward = np.concatenate([own_re, own_im, rim_re, pad, rim_im, pad], axis=1)

    low = np.array([(a, b) for a in range(groups) for b in range(members)])

    def twiddle(cells):
        return (
            2.0 * np.pi * np.outer(low[:, 0], cells[:, 0]) / waves_x
            + 2.0 * np.pi * np.outer(low[:, 1], cells[:, 1]) / waves_y
        )

    angle = twiddle(own)
    rim_angle = np.pad(twiddle(rim), ((0, 0), (0, HALF - len(rim))))
    twist = np.concatenate(
        [
            np.cos(angle),
            np.sin(angle),
            np.cos(rim_angle),
            np.cos(rim_angle),
            -np.sin(rim_angle),
            np.sin(rim_angle),
        ],
        axis=1,
    )
    wave_x = low[:, None, 0] + groups * high[None, :, 0]
    wave_y = low[:, None, 1] + members * high[None, :, 1]
    eigen = (2.0 - 2.0 * np.cos(2.0 * np.pi * wave_x / waves_x)) / 16.0
    eigen = eigen + (2.0 - 2.0 * np.cos(2.0 * np.pi * wave_y / waves_y)) / 16.0
    height = 2.0 - 2.0 * np.cos(np.pi * np.arange(1, layers + 1) / (layers + 1))
    height = np.broadcast_to(height[:, None], (layers, LANES))
    return [np.asarray(t, np.float32) for t in (forward, backward, twist, eigen, height)]


def lanes_of(tile):
    return pl.ds(tile * LANES, LANES)


def iota(axis):
    return lax.broadcasted_iota(jnp.int32, (SUBS, LANES), axis)


def roll_z(value, step):
    return pltpu.roll(value, step % LANES, 1)


def roll_y(value, step):
    return pltpu.roll(value, step % SUBS, 0)


def ends_of(tiles, lane):
    return jnp.where(lane < HALF, tiles[0], tiles[-1])


def vertical_pair(tiles, edge, lane):
    below = [roll_z(t, 1) for t in tiles]
    above = [roll_z(t, -1) for t in tiles]
    first, last = lane == 0, lane == LANES - 1
    out = []
    for k in range(len(tiles)):
        down = jnp.where(first, edge if k == 0 else below[k - 1], below[k])
        up = jnp.where(last, edge if k + 1 == len(tiles) else above[k + 1], above[k])
        out.append(down + up)
    return out


def row_pair(tiles, index, sub):
    first, last = sub == 0, sub == SUBS - 1
    if index == 0:
        return tiles[1] + jnp.where(first, tiles[4], roll_y(tiles[3], 1))
    if index == 3:
        return tiles[2] + jnp.where(last, tiles[4], roll_y(tiles[0], -1))
    if index == 4:
        inner = jnp.where(first, tiles[0], roll_y(tiles[4], 1))
        return inner + jnp.where(last, tiles[3], roll_y(tiles[4], -1))
    return tiles[index - 1] + tiles[index + 1]


def side_flags():
    groups, members = lax.axis_size("group"), lax.axis_size("dev")
    group, member = lax.axis_index("group"), lax.axis_index("dev")
    as_float = lambda test: jnp.where(test, 1.0, 0.0).astype(jnp.float32)
    return (
        as_float(group > 0),
        as_float(group < groups - 1),
        as_float(member > 0),
        as_float(member < members - 1),
    )


def swap_pairs(count):
    first = [(i, i ^ 1) for i in range(count) if (i ^ 1) < count]
    second = [(i, ((i + 1) ^ 1) - 1) for i in range(count)]
    return first, [(i, j) for i, j in second if 0 <= j < count]


def swap(pair, axis):
    first, second = swap_pairs(lax.axis_size(axis))
    return lax.ppermute(pair[0], axis, first), lax.ppermute(pair[1], axis, second)


def slab_list():
    out = [(0, c, d) for c in range(2) for d in range(FIELD_HALO)]
    out += [(1, c, d) for c in range(2) for d in range(DATA_HALO)]
    return out + [(2, 0, d) for d in range(DATA_HALO)]


def coarse_kernel(
    shape,
    f_hbm, s_hbm, w_hbm, basis_ref,
    out_ref, xa_hbm, xb_hbm, ya_hbm, yb_hbm,
    f_ref, s_ref, w_ref, ce_ref, sums_ref, rows_ref, pack_ref,
    in_sem, x_sem, y_sem,
):
    nx, ny, nz = shape
    tiles = nz // LANES
    blocks = nx // BLOCK
    chunk = BLOCK * ny
    own = blocks * SUBS
    lane, sub = iota(1), iota(0)

    def fetch(i):
        rows = pl.ds(pl.multiple_of(i * chunk, chunk), chunk)
        return [
            pltpu.make_async_copy(src.at[:, rows, lanes_of(k)], dst.at[:, k, rows], in_sem.at[a, k, i])
            for a, (src, dst) in enumerate(((f_hbm, f_ref), (s_hbm, s_ref), (w_hbm, w_ref)))
            for k in range(tiles)
        ]

    def start(i, carry):
        for copy in fetch(i):
            copy.start()
        return carry

    lax.fori_loop(0, blocks, start, 0)
    zero = jnp.zeros((SUBS, LANES), jnp.float32)
    for c in range(2):
        for k in range(tiles):
            sums_ref[c, 0, :, lanes_of(k)] = zero

    def block(i, before):
        for copy in fetch(i):
            copy.wait()
        total = [[None] * tiles for _ in range(2)]
        by_row = [[[None] * tiles for _ in range(2)] for _ in range(BLOCK)]
        by_plane = [[[None] * tiles for _ in range(2)] for _ in range(BLOCK)]
        robin = [None, None]

        def add(store, key, value):
            store[key] = value if store[key] is None else store[key] + value

        for x in range(BLOCK):
            for t in range(BLOCK):
                rows = pl.ds(i * chunk + x * ny + t, SUBS, stride=BLOCK)
                wave = [w_ref[0, k, rows, :] for k in range(tiles)]
                absorb = jnp.sqrt(ends_of(wave, lane))
                ends = []
                for c in range(2):
                    cells = [f_ref[c, k, rows, :] for k in range(tiles)]
                    for k in range(tiles):
                        value = s_ref[c, k, rows, :] + (wave[k] - 2.0) * cells[k]
                        add(total[c], k, value)
                        add(by_row[t][c], k, cells[k])
                        add(by_plane[x][c], k, cells[k])
                    ends.append(ends_of(cells, lane))
                add(robin, 0, absorb * ends[1])
                add(robin, 1, absorb * ends[0])
        after = []
        for c in range(2):
            every = [sum(by_row[t][c][k] for t in range(1, BLOCK)) + by_row[0][c][k] for k in range(tiles)]
            edge = ends_of(every, lane)
            edge = edge - robin[0] if c == 0 else edge + robin[1]
            upright = vertical_pair(every, edge, lane)
            for k in range(tiles):
                top, bottom = by_row[0][c][k], by_row[BLOCK - 1][c][k]
                down = jnp.where(sub == 0, 0.0, roll_y(bottom, 1))
                up = jnp.where(sub == SUBS - 1, 0.0, roll_y(top, -1))
                value = total[c][k] + upright[k] + ((down - bottom) + (up - top))
                value = value - by_plane[0][c][k] - by_plane[BLOCK - 1][c][k]
                sums_ref[c, i + 1, :, lanes_of(k)] = value + before[c * tiles + k]
                earlier = sums_ref[c, i, :, lanes_of(k)]
                sums_ref[c, i, :, lanes_of(k)] = earlier + by_plane[0][c][k]
                tile = pl.ds(pl.multiple_of(i * SUBS, SUBS), SUBS)
                rows_ref[c, 0, k, tile, :] = top
                rows_ref[c, 1, k, tile, :] = bottom
                after.append(by_plane[BLOCK - 1][c][k])
        return tuple(after)

    beyond = lax.fori_loop(0, blocks, block, (zero,) * (2 * tiles))

    sources = (f_ref, s_ref, w_ref)
    x_odd = lax.rem(lax.axis_index("group"), 2)
    y_odd = lax.rem(lax.axis_index("dev"), 2)
    x_copies = []
    for side, target in enumerate((xa_hbm, xb_hbm)):
        high = (x_odd == 0) if side == 0 else (x_odd == 1)
        for slab, (array, c, d) in enumerate(slab_list()):
            plane = jnp.where(high, nx - 1 - d, d)
            rows = pl.ds(pl.multiple_of(plane * ny, ny), ny)
            copy = pltpu.make_async_copy(
                sources[array].at[c, :, rows], target.at[slab], x_sem.at[side, slab]
            )
            copy.start()
            x_copies.append(copy)

    def gather(j, carry):
        for side in range(2):
            high = (y_odd == 0) if side == 0 else (y_odd == 1)
            for slab, (array, c, d) in enumerate(slab_list()):
                row = jnp.where(high, ny - 1 - d, d)
                for k in range(tiles):
                    rows = pl.ds(j * SUBS * ny + row, SUBS, stride=ny)
                    value = sources[array][c, k, rows, :]
                    pack_ref[side, slab, k, pl.ds(pl.multiple_of(j * SUBS, SUBS), SUBS), :] = value
        return carry

    lax.fori_loop(0, nx // SUBS, gather, 0)
    y_copies = []
    for side, target in enumerate((ya_hbm, yb_hbm)):
        copy = pltpu.make_async_copy(pack_ref.at[side], target, y_sem.at[side])
        copy.start()
        y_copies.append(copy)

    low_x, high_x, low_y, high_y = side_flags()
    for c in range(2):
        for k in range(tiles):
            z = lanes_of(k)
            for i in range(blocks):
                ce_ref[pl.ds(c * own + i * SUBS, SUBS), z] = sums_ref[c, i + 1, :, z]
            rim = 2 * own + c * HALF
            ce_ref[pl.ds(rim, SUBS), z] = sums_ref[c, 0, :, z] * low_x
            ce_ref[pl.ds(rim + SUBS, SUBS), z] = beyond[c * tiles + k] * high_x
            base = rim + 2 * SUBS
            for i in range(0, blocks, SUBS):
                top = pl.ds(i * SUBS, SUBS, stride=SUBS)
                bottom = pl.ds(i * SUBS + SUBS - 1, SUBS, stride=SUBS)
                ce_ref[pl.ds(base + i, SUBS), z] = rows_ref[c, 0, k, top, :] * low_y
                ce_ref[pl.ds(base + blocks + i, SUBS), z] = rows_ref[c, 1, k, bottom, :] * high_y
            rest = HALF - 2 * SUBS - 2 * blocks
            ce_ref[pl.ds(base + 2 * blocks, rest), z] = jnp.zeros((rest, LANES), jnp.float32)
    modes = lax.dot_general(
        basis_ref[...], ce_ref[...], (((1,), (1,)), ((), ())),
        precision=HIGHEST, preferred_element_type=jnp.float32,
    )
    out_ref[...] = modes * (1.0 / (BLOCK * BLOCK))
    for copy in x_copies + y_copies:
        copy.wait()


def coarse_modes(field, source, wave_sq, basis):
    _, nx, ny, nz = field.shape
    blocks = nx // BLOCK
    width = 2 * blocks * SUBS + 2 * HALF
    f32 = jnp.float32
    tiles = nz // LANES
    x_shape = jax.ShapeDtypeStruct((SLABS, tiles, ny, LANES), f32)
    y_shape = jax.ShapeDtypeStruct((SLABS, tiles, nx, LANES), f32)
    return pl.pallas_call(
        functools.partial(coarse_kernel, (nx, ny, nz)),
        out_shape=(jax.ShapeDtypeStruct((nz, width), f32), x_shape, x_shape, y_shape, y_shape),
        in_specs=[pl.BlockSpec(memory_space=ANY)] * 3 + [pl.BlockSpec(memory_space=VMEM)],
        out_specs=(pl.BlockSpec(memory_space=VMEM),) + (pl.BlockSpec(memory_space=ANY),) * 4,
        scratch_shapes=[
            VMEM((2, tiles, nx * ny, LANES), f32),
            VMEM((2, tiles, nx * ny, LANES), f32),
            VMEM((1, tiles, nx * ny, LANES), f32),
            VMEM((width, nz), f32),
            VMEM((2, blocks + 1, SUBS, nz), f32),
            VMEM((2, 2, tiles, blocks * SUBS, LANES), f32),
            VMEM((2, SLABS, tiles, nx, LANES), f32),
            pltpu.SemaphoreType.DMA((3, tiles, blocks)),
            pltpu.SemaphoreType.DMA((2, SLABS)),
            pltpu.SemaphoreType.DMA((2,)),
        ],
        compiler_params=pltpu.CompilerParams(vmem_limit_bytes=VMEM_LIMIT),
        name="coarse_modes",
    )(
        field.reshape(2, nx * ny, nz),
        source.reshape(2, nx * ny, nz),
        wave_sq.reshape(1, nx * ny, nz),
        basis,
    )


def add_cells(a, b):
    return tuple(x + y for x, y in zip(a, b))


def sub_cells(a, b):
    return tuple(x - y for x, y in zip(a, b))


def turn_cells(a, flip):
    return (-a[1], a[0], flip * pltpu.roll(a[2], HALF, 1))


def scale_cells(a, real, imag, flip):
    if abs(imag) < 1e-12:
        return a if real == 1.0 else tuple(real * x for x in a)
    turned = turn_cells(a, flip)
    if abs(real) < 1e-12:
        return tuple(imag * x for x in turned)
    return tuple(real * x + imag * y for x, y in zip(a, turned))


def butterflies(items, sign, flip):
    count = len(items)
    if count == 1:
        return items
    if count % 2:
        out = []
        for k in range(count):
            acc = items[0]
            for j in range(1, count):
                angle = sign * 2.0 * math.pi * (j * k % count) / count
                acc = add_cells(acc, scale_cells(items[j], math.cos(angle), math.sin(angle), flip))
            out.append(acc)
        return out
    even = butterflies(items[0::2], sign, flip)
    odd = butterflies(items[1::2], sign, flip)
    low, high = [], []
    for k in range(count // 2):
        angle = sign * 2.0 * math.pi * k / count
        real, imag = math.cos(angle), math.sin(angle)
        if abs(real) < 1e-12:
            turned = turn_cells(odd[k], flip)
            plus, minus = (add_cells, sub_cells) if imag > 0 else (sub_cells, add_cells)
            low.append(plus(even[k], turned))
            high.append(minus(even[k], turned))
        else:
            turned = scale_cells(odd[k], real, imag, flip)
            low.append(add_cells(even[k], turned))
            high.append(sub_cells(even[k], turned))
    return low + high


def solve_kernel(
    groups, members, local,
    shift_ref, x_ref, forward_ref, backward_ref, twist_ref, eigen_ref, height_ref,
    out_ref, one_ref, two_ref,
):
    count = groups * members
    lane = lax.broadcasted_iota(jnp.int32, (local, LANES), 1)
    flip = jnp.where(lane < HALF, -1.0, 1.0).astype(jnp.float32)

    def load(ref, index):
        rows = pl.ds(index * local, local)
        return tuple(ref[rows, lanes_of(k)] for k in range(3))

    def save(ref, index, cells):
        rows = pl.ds(index * local, local)
        for k in range(3):
            ref[rows, lanes_of(k)] = cells[k]

    def twist(index, cells, sign):
        cos, sin, rim_cos, rim_sin = (twist_ref[pl.ds(index, 1), lanes_of(k)] for k in range(4))
        spun = pltpu.roll(cells[2], HALF, 1)
        if sign < 0:
            return (
                cells[0] * cos + cells[1] * sin,
                cells[1] * cos - cells[0] * sin,
                cells[2] * rim_cos - spun * rim_sin,
            )
        return (
            cells[0] * cos - cells[1] * sin,
            cells[1] * cos + cells[0] * sin,
            cells[2] * rim_cos + spun * rim_sin,
        )

    for g in range(groups):
        items = butterflies([load(x_ref, g * members + d) for d in range(members)], -1, flip)
        for d in range(members):
            save(one_ref, g * members + d, items[d])
    for d in range(members):
        items = butterflies([load(one_ref, g * members + d) for g in range(groups)], -1, flip)
        for g in range(groups):
            save(two_ref, g * members + d, twist(g * members + d, items[g], -1))
    spectrum = jnp.dot(
        two_ref[...], forward_ref[...], precision=HIGHEST, preferred_element_type=jnp.float32
    )
    one_ref[:, 0 : 2 * LANES] = spectrum
    shift = shift_ref[0]
    imag = -DAMPING * shift
    me = lax.axis_index("group") * members + lax.axis_index("dev")
    height = height_ref[pl.ds(me * local, local), :]
    for i in range(count):
        rows = pl.ds(i * local, local)
        real = (eigen_ref[pl.ds(i, 1), :] + height) - shift
        inverse = 1.0 / (real * real + imag * imag)
        up, low = one_ref[rows, lanes_of(0)], one_ref[rows, lanes_of(1)]
        two_ref[rows, lanes_of(0)] = (up * real + low * imag) * inverse
        two_ref[rows, lanes_of(1)] = (low * real - up * imag) * inverse
    cells = jnp.dot(
        two_ref[:, 0 : 2 * LANES], backward_ref[...],
        precision=HIGHEST, preferred_element_type=jnp.float32,
    )
    one_ref[...] = cells
    for d in range(members):
        items = [twist(g * members + d, load(one_ref, g * members + d), 1) for g in range(groups)]
        items = butterflies(items, 1, flip)
        for g in range(groups):
            save(two_ref, g * members + d, items[g])
    for g in range(groups):
        items = butterflies([load(two_ref, g * members + d) for d in range(members)], 1, flip)
        for d in range(members):
            save(out_ref, g * members + d, items[d])


def solve_modes(gathered, shift_sq, tables):
    groups, members = lax.axis_size("group"), lax.axis_size("dev")
    local = gathered.shape[0] // (groups * members)
    f32 = jnp.float32
    return pl.pallas_call(
        functools.partial(solve_kernel, groups, members, local),
        out_shape=jax.ShapeDtypeStruct(gathered.shape, f32),
        in_specs=[pl.BlockSpec(memory_space=pltpu.SMEM)] + [pl.BlockSpec(memory_space=VMEM)] * 6,
        out_specs=pl.BlockSpec(memory_space=VMEM),
        scratch_shapes=[VMEM(gathered.shape, f32), VMEM(gathered.shape, f32)],
        compiler_params=pltpu.CompilerParams(vmem_limit_bytes=16 * 1024 * 1024),
        name="solve_modes",
    )(shift_sq, gathered, *tables)


def rim_kernel(nx, ya_ref, yb_ref, rim_ref, ma_ref, mb_ref):
    tiles = ya_ref.shape[1]
    x_odd = lax.rem(lax.axis_index("group"), 2)
    y_odd = lax.rem(lax.axis_index("dev"), 2)
    rim_ref[...] = jnp.zeros_like(rim_ref)
    slot = {0: 0, 1: 2, 2: 4}

    def scatter(j, carry):
        for side, ref in enumerate((ya_ref, yb_ref)):
            high = (y_odd == 0) if side == 0 else (y_odd == 1)
            for slab, (array, c, d) in enumerate(slab_list()):
                row = jnp.where(high, SUBS - 1 - d, d)
                for k in range(tiles):
                    value = ref[slab, k, pl.ds(pl.multiple_of(j * SUBS, SUBS), SUBS), :]
                    rows = pl.ds(j * SUBS * SUBS + row, SUBS, stride=SUBS)
                    rim_ref[slot[array] + c, k, rows, :] = value
        return carry

    lax.fori_loop(0, nx // SUBS, scatter, 0)
    for side, ref in enumerate((ma_ref, mb_ref)):
        high = (x_odd == 0) if side == 0 else (x_odd == 1)
        near = jnp.where(high, nx - 1, 0)
        next_one = jnp.where(high, nx - 2, 1)
        for index, (array, plane) in enumerate(
            ((0, near), (1, near), (0, next_one), (1, next_one), (2, near), (3, near), (4, near))
        ):
            rows = pl.ds(pl.multiple_of(plane * SUBS, SUBS), SUBS)
            ref[index] = rim_ref[array, :, rows, :]


def rim_rows(first, second):
    _, tiles, nx, _ = first.shape
    f32 = jnp.float32
    corner = jax.ShapeDtypeStruct((7, tiles, SUBS, LANES), f32)
    return pl.pallas_call(
        functools.partial(rim_kernel, nx),
        out_shape=(jax.ShapeDtypeStruct((5, tiles, nx * SUBS, LANES), f32), corner, corner),
        in_specs=[pl.BlockSpec(memory_space=VMEM)] * 2,
        out_specs=(pl.BlockSpec(memory_space=VMEM),) * 3,
        compiler_params=pltpu.CompilerParams(vmem_limit_bytes=16 * 1024 * 1024),
        name="rim_rows",
    )(first, second)


def first_kernel(
    shape,
    f_hbm, s_hbm, w_hbm, rim_hbm, xa_hbm, xb_hbm, ma_hbm, mb_hbm,
    v_ref, sp_ref, wt_ref, ab_ref,
    f_ref, s_ref, w_ref, rim_ref, xs_ref, ms_ref, ext_ref,
    sem, rim_sem, side_sem,
):
    nx, ny, nz = shape
    tiles = nz // LANES
    chunks = nx // SUBS
    chunk = SUBS * ny
    lane, sub = iota(1), iota(0)
    x_odd = lax.rem(lax.axis_index("group"), 2)
    low_x, high_x, low_y, high_y = side_flags()
    rim_mask = jnp.where(sub < SUBS // 2, low_y, high_y)

    def fetch(i):
        rows = pl.ds(pl.multiple_of(i * chunk, chunk), chunk)
        near = pl.ds(pl.multiple_of(i * SUBS * SUBS, SUBS * SUBS), SUBS * SUBS)
        copies = [
            pltpu.make_async_copy(src.at[:, rows, lanes_of(k)], dst.at[:, k, rows], sem.at[a, k, i])
            for a, (src, dst) in enumerate(((f_hbm, f_ref), (s_hbm, s_ref), (w_hbm, w_ref)))
            for k in range(tiles)
        ]
        return copies + [
            pltpu.make_async_copy(rim_hbm.at[:, :, near], rim_ref.at[:, :, near], rim_sem.at[i])
        ]

    def start(i, carry):
        for copy in fetch(i):
            copy.start()
        return carry

    lax.fori_loop(0, chunks, start, 0)
    high_first = jnp.where(x_odd == 0, 1, 0)
    sides = []
    for index, (ref, target, side) in enumerate(
        (
            (xa_hbm, xs_ref, high_first),
            (xb_hbm, xs_ref, 1 - high_first),
            (ma_hbm, ms_ref, high_first),
            (mb_hbm, ms_ref, 1 - high_first),
        )
    ):
        copy = pltpu.make_async_copy(ref, target.at[side], side_sem.at[index])
        copy.start()
        sides.append(copy)

    def settle(q, t, source, wave, mask):
        for k in range(tiles):
            weight = RELAX / (6.0 - wave[k])
            if mask is not None:
                weight = weight * mask
            wt_ref[q, t, :, lanes_of(k)] = weight
            for c in range(2):
                sp_ref[c, q, t, :, lanes_of(k)] = weight * source[c][k]
        ab_ref[q, t] = jnp.sqrt(ends_of(wave, lane))

    depth = FIELD_HALO
    skip = DATA_HALO

    def own(i, carry):
        for copy in fetch(i):
            copy.wait()

        def plane(j, inner):
            x = i * SUBS + j
            for t in range(BLOCK):
                rows = pl.ds(x * ny + t, SUBS, stride=BLOCK)
                for c in range(2):
                    for k in range(tiles):
                        ext_ref[c, x + depth, t, :, lanes_of(k)] = f_ref[c, k, rows, :]
                source = [[s_ref[c, k, rows, :] for k in range(tiles)] for c in range(2)]
                settle(x + skip, t, source, [w_ref[0, k, rows, :] for k in range(tiles)], None)
            rows = pl.ds(pl.multiple_of(x * SUBS, SUBS), SUBS)
            for c in range(2):
                for k in range(tiles):
                    ext_ref[c, x + depth, BLOCK, :, lanes_of(k)] = rim_ref[c, k, rows, :]
            source = [[rim_ref[2 + c, k, rows, :] for k in range(tiles)] for c in range(2)]
            wave = [rim_ref[4, k, rows, :] for k in range(tiles)]
            settle(x + skip, BLOCK, source, wave, rim_mask)
            return inner

        return lax.fori_loop(0, SUBS, plane, carry)

    lax.fori_loop(0, chunks, own, 0)
    for copy in sides:
        copy.wait()
    slabs = {key: index for index, key in enumerate(slab_list())}
    zero = jnp.zeros((SUBS, LANES), jnp.float32)
    for side, flag in ((0, low_x), (1, high_x)):
        for d in range(FIELD_HALO):
            x = nx + d if side else -1 - d
            for t in range(BLOCK):
                rows = pl.ds(t, SUBS, stride=BLOCK)
                for c in range(2):
                    for k in range(tiles):
                        ext_ref[c, x + depth, t, :, lanes_of(k)] = xs_ref[side, slabs[(0, c, d)], k, rows, :]
                if d < DATA_HALO:
                    source = [
                        [xs_ref[side, slabs[(1, c, d)], k, rows, :] for k in range(tiles)]
                        for c in range(2)
                    ]
                    wave = [xs_ref[side, slabs[(2, 0, d)], k, rows, :] for k in range(tiles)]
                    settle(x + skip, t, source, wave, flag)
            for c in range(2):
                for k in range(tiles):
                    cells = ms_ref[side, 2 * d + c, k] if d < 2 else zero
                    ext_ref[c, x + depth, BLOCK, :, lanes_of(k)] = cells
            if d == 0:
                source = [[ms_ref[side, 4 + c, k] for k in range(tiles)] for c in range(2)]
                wave = [ms_ref[side, 6, k] for k in range(tiles)]
                settle(x + skip, BLOCK, source, wave, rim_mask * flag)
            elif d < DATA_HALO:
                settle(x + skip, BLOCK, [[zero] * tiles] * 2, [zero] * tiles, rim_mask * flag)

    def step(q, carry):
        relax_plane(
            ext_ref, q + 1, BLOCK + 1, tiles, lane, sub,
            lambda t: [wt_ref[q, t, :, lanes_of(k)] for k in range(tiles)],
            lambda c, t: [sp_ref[c, q, t, :, lanes_of(k)] for k in range(tiles)],
            lambda t: ab_ref[q, t],
            functools.partial(store_tile, v_ref, q),
        )
        return carry

    lax.fori_loop(0, nx + 2 * skip, step, 0)


def store_tile(ref, q, c, t, k, value):
    ref[c, q, t, :, lanes_of(k)] = value


def relax_plane(ref, p, count, tiles, lane, sub, weights, sources, absorbs, store):
    centre = [
        [[ref[c, p, t, :, lanes_of(k)] for k in range(tiles)] for t in range(BLOCK + 1)]
        for c in range(2)
    ]
    for t in range(count):
        ends = [ends_of(centre[c][t], lane) for c in range(2)]
        absorb = absorbs(t)
        weight = weights(t)
        for c in range(2):
            other = absorb * ends[1 - c]
            edge = ends[c] - other if c == 0 else ends[c] + other
            upright = vertical_pair(centre[c][t], edge, lane)
            source = sources(c, t)
            for k in range(tiles):
                beside = ref[c, p - 1, t, :, lanes_of(k)] + ref[c, p + 1, t, :, lanes_of(k)]
                column = [centre[c][s][k] for s in range(BLOCK + 1)]
                beside = beside + row_pair(column, t, sub) + upright[k]
                value = (1.0 - RELAX) * centre[c][t][k] + (source[k] + weight[k] * beside)
                store(c, t, k, value)


def first_sweep(field, source, wave_sq, rim, planes, corners):
    _, nx, ny, nz = field.shape
    f32 = jnp.float32
    wide = nx + 2 * DATA_HALO
    tall = BLOCK + 1
    tiles = nz // LANES
    chunks = nx // SUBS
    return pl.pallas_call(
        functools.partial(first_kernel, (nx, ny, nz)),
        out_shape=(
            jax.ShapeDtypeStruct((2, wide, tall, SUBS, nz), f32),
            jax.ShapeDtypeStruct((2, wide, tall, SUBS, nz), f32),
            jax.ShapeDtypeStruct((wide, tall, SUBS, nz), f32),
            jax.ShapeDtypeStruct((wide, tall, SUBS, LANES), f32),
        ),
        in_specs=[pl.BlockSpec(memory_space=ANY)] * 8,
        out_specs=(pl.BlockSpec(memory_space=VMEM),) * 4,
        scratch_shapes=[
            VMEM((2, tiles, nx * ny, LANES), f32),
            VMEM((2, tiles, nx * ny, LANES), f32),
            VMEM((1, tiles, nx * ny, LANES), f32),
            VMEM((5, tiles, nx * SUBS, LANES), f32),
            VMEM((2, SLABS, tiles, ny, LANES), f32),
            VMEM((2, 7, tiles, SUBS, LANES), f32),
            VMEM((2, nx + 2 * FIELD_HALO, tall, SUBS, nz), f32),
            pltpu.SemaphoreType.DMA((3, tiles, chunks)),
            pltpu.SemaphoreType.DMA((chunks,)),
            pltpu.SemaphoreType.DMA((4,)),
        ],
        compiler_params=pltpu.CompilerParams(vmem_limit_bytes=VMEM_LIMIT),
        name="first_sweep",
    )(
        field.reshape(2, nx * ny, nz),
        source.reshape(2, nx * ny, nz),
        wave_sq.reshape(1, nx * ny, nz),
        rim, *planes, *corners,
    )


def last_kernel(
    shape,
    modes_ref, basis_ref, v_ref, sp_ref, wt_ref, ab_ref,
    out_hbm,
    es_ref, em_ref, eh_ref, yt_ref, one_ref, two_ref, stage_ref, sem,
):
    nx, ny, nz = shape
    tiles = nz // LANES
    blocks = nx // BLOCK
    own = blocks * SUBS
    skip = DATA_HALO
    lane, sub = iota(1), iota(0)
    low_x, high_x, low_y, high_y = side_flags()
    rim_mask = jnp.where(sub < SUBS // 2, low_y, high_y)
    es_ref[...] = lax.dot_general(
        modes_ref[...], basis_ref[...], (((0,), (0,)), ((), ())),
        precision=HIGHEST, preferred_element_type=jnp.float32,
    )

    def rim_tile(low, high, z):
        low = jnp.broadcast_to(es_ref[pl.ds(low, 1), z], (SUBS, LANES))
        high = jnp.broadcast_to(es_ref[pl.ds(high, 1), z], (SUBS, LANES))
        return jnp.where(sub < SUBS // 2, low, high) * rim_mask

    for c in range(2):
        for k in range(tiles):
            z = lanes_of(k)
            base = 2 * own + c * HALF
            for i in range(blocks):
                em_ref[c, i + 1, :, z] = es_ref[pl.ds(c * own + i * SUBS, SUBS), z]
                row = base + 2 * SUBS + i
                eh_ref[c, i + 1, :, z] = rim_tile(row, row + blocks, z)
            em_ref[c, 0, :, z] = es_ref[pl.ds(base, SUBS), z] * low_x
            em_ref[c, blocks + 1, :, z] = es_ref[pl.ds(base + SUBS, SUBS), z] * high_x
            row = base + 2 * SUBS + 2 * blocks
            eh_ref[c, 0, :, z] = rim_tile(row, row + 1, z) * low_x
            eh_ref[c, blocks + 1, :, z] = rim_tile(row + 2, row + 3, z) * high_x

    first, last = sub == 0, sub == SUBS - 1

    def column(i, carry):
        for c in range(2):
            cells = [em_ref[c, i, :, lanes_of(k)] for k in range(tiles)]
            rims = [eh_ref[c, i, :, lanes_of(k)] for k in range(tiles)]
            upright = vertical_pair(cells, ends_of(cells, lane), lane)
            rim_upright = vertical_pair(rims, ends_of(rims, lane), lane)
            for k in range(tiles):
                z = lanes_of(k)
                down = jnp.where(first, rims[k], roll_y(cells[k], 1))
                up = jnp.where(last, rims[k], roll_y(cells[k], -1))
                inner = upright[k] + cells[k]
                yt_ref[c, i, 0, :, z] = inner + down
                yt_ref[c, i, 1, :, z] = inner + cells[k]
                yt_ref[c, i, 2, :, z] = inner + up
                beside = jnp.where(first | last, cells[k], rims[k])
                yt_ref[c, i, 3, :, z] = rim_upright[k] + rims[k] + beside
        return carry

    lax.fori_loop(0, blocks + 2, column, 0)
    kinds = (0, 1, 1, 2, 3)
    blank = jnp.zeros((SUBS, LANES), jnp.float32)

    def correct(q, carry):
        at = q + BLOCK - skip
        i = lax.shift_right_logical(at, 2)
        spot = at & (BLOCK - 1)
        near = i + jnp.where(spot == BLOCK - 1, 1, 0) - jnp.where(spot == 0, 1, 0)
        for rim in range(2):
            ref = eh_ref if rim else em_ref
            cells = [[ref[c, i, :, lanes_of(k)] for k in range(tiles)] for c in range(2)]
            across = [
                [cells[c][k] + ref[c, near, :, lanes_of(k)] for k in range(tiles)] for c in range(2)
            ]
            fade = [[(1.0 - RELAX) * cells[c][k] for k in range(tiles)] for c in range(2)]
            ends = [ends_of(cells[c], lane) for c in range(2)]
            for t in (BLOCK,) if rim else range(BLOCK):
                absorb = ab_ref[q, t]
                for c in range(2):
                    bend = absorb * ends[1 - c]
                    bend = -bend if c == 0 else bend
                    for k in range(tiles):
                        z = lanes_of(k)
                        beside = yt_ref[c, i, kinds[t], :, z] + across[c][k]
                        if k == 0:
                            beside = beside + jnp.where(lane == 0, bend, blank)
                        if k == tiles - 1:
                            beside = beside + jnp.where(lane == LANES - 1, bend, blank)
                        value = (v_ref[c, q, t, :, z] + fade[c][k]) + wt_ref[q, t, :, z] * beside
                        one_ref[c, q, t, :, z] = value
        return carry

    lax.fori_loop(0, nx + 2 * skip, correct, 0)

    def loads(q):
        return (
            lambda t: [wt_ref[q, t, :, lanes_of(k)] for k in range(tiles)],
            lambda c, t: [sp_ref[c, q, t, :, lanes_of(k)] for k in range(tiles)],
            lambda t: ab_ref[q, t],
        )

    def second(q, carry):
        relax_plane(
            one_ref, q, BLOCK + 1, tiles, lane, sub, *loads(q),
            functools.partial(store_tile, two_ref, q),
        )
        return carry

    lax.fori_loop(1, nx + 2 * skip - 1, second, 0)

    chunk = SUBS * ny

    def send(i):
        rows = pl.ds(pl.multiple_of(i * chunk, chunk), chunk)
        return [
            pltpu.make_async_copy(stage_ref.at[:, k, rows], out_hbm.at[:, rows, lanes_of(k)], sem.at[k, i])
            for k in range(tiles)
        ]

    def third(i, carry):
        def plane(j, inner):
            x = i * SUBS + j

            def store(c, t, k, value):
                stage_ref[c, k, pl.ds(x * ny + t, SUBS, stride=BLOCK), :] = value

            relax_plane(
                two_ref, x + skip, BLOCK, tiles, lane, sub, *loads(x + skip), store
            )
            return inner

        carry = lax.fori_loop(0, SUBS, plane, carry)
        for copy in send(i):
            copy.start()
        return carry

    lax.fori_loop(0, nx // SUBS, third, 0)

    def finish(i, carry):
        for copy in send(i):
            copy.wait()
        return carry

    lax.fori_loop(0, nx // SUBS, finish, 0)


def last_sweeps(modes, basis, parts, shape):
    _, nx, ny, nz = shape
    f32 = jnp.float32
    wide = nx + 2 * DATA_HALO
    tall = BLOCK + 1
    blocks = nx // BLOCK
    out = pl.pallas_call(
        functools.partial(last_kernel, (nx, ny, nz)),
        out_shape=jax.ShapeDtypeStruct((2, nx * ny, nz), f32),
        in_specs=[pl.BlockSpec(memory_space=VMEM)] * 6,
        out_specs=pl.BlockSpec(memory_space=ANY),
        scratch_shapes=[
            VMEM((modes.shape[1], nz), f32),
            VMEM((2, blocks + 2, SUBS, nz), f32),
            VMEM((2, blocks + 2, SUBS, nz), f32),
            VMEM((2, blocks + 2, 4, SUBS, nz), f32),
            VMEM((2, wide, tall, SUBS, nz), f32),
            VMEM((2, wide, tall, SUBS, nz), f32),
            VMEM((2, nz // LANES, nx * ny, LANES), f32),
            pltpu.SemaphoreType.DMA((nz // LANES, nx // SUBS)),
        ],
        compiler_params=pltpu.CompilerParams(vmem_limit_bytes=VMEM_LIMIT),
        name="last_sweeps",
    )(modes, basis, *parts)
    return out.reshape(shape)


def body(tables, field_now, source, wavenumber_sq, shift_sq):
    everyone = ("group", "dev")
    basis, spectral = jnp.asarray(tables[0]), [jnp.asarray(t) for t in tables[1:]]
    modes, xa, xb, ya, yb = coarse_modes(field_now, source, wavenumber_sq, basis)
    gathered = lax.all_to_all(modes, everyone, split_axis=0, concat_axis=0, tiled=True)
    rows = swap((ya, yb), "dev")
    planes = swap((xa, xb), "group")
    solved = solve_modes(gathered, shift_sq, spectral)
    returned = lax.all_to_all(solved, everyone, split_axis=0, concat_axis=0, tiled=True)
    rim, ma, mb = rim_rows(*rows)
    corners = swap((ma, mb), "group")
    parts = first_sweep(field_now, source, wavenumber_sq, rim, planes, corners)
    return last_sweeps(returned, basis, parts, field_now.shape)


def solution(mesh):
    groups, members = mesh.shape["group"], mesh.shape["dev"]

    def whole(field_now, source, wavenumber_sq, shift_sq):
        _, nx, ny, nz = field_now.shape
        cells_x, cells_y = nx // groups // BLOCK, ny // members // BLOCK
        tables = [np.asarray(vertical_basis(nz), np.float32)]
        tables += spectral_tables(groups, members, cells_x, cells_y, nz)
        return jax.shard_map(
            functools.partial(body, tables),
            mesh=mesh,
            in_specs=(
                P(None, "group", "dev", None),
                P(None, "group", "dev", None),
                P("group", "dev", None),
                P(),
            ),
            out_specs=P(None, "group", "dev", None),
            check_vma=False,
        )(field_now, source, wavenumber_sq, shift_sq)

    return whole
```
